256 devices in a mesh: section: 8 (over y, core), node: 32 (over x, z).
Axes of the slice: x: 4, y: 4, z: 8, core: 2. Of those that a mesh axis runs over, the one named last changes fastest.
Arguments:
- acts: bfloat16 [8, 3, 8192, 512], P('section', None, 'node'), may hold values from -6 to 6
- top_grad: bfloat16 [3, 8192, 512], P(None, 'node'), may hold values from -6 to 6
- w_in: bfloat16 [8, 512, 1024], P('section'), may hold values from -0.25 to 0.25
- w_out: bfloat16 [8, 1024, 512], P('section'), may hold values from -0.1875 to 0.1875
- tile_table: bfloat16 [3, 256, 128, 128], P(None, 'node'), may hold values from -0.25 to 0.25
- tile_rows: int32 [3, 256], P(None, 'node'), may hold values from 0 to 1
- tile_cols: int32 [3, 256], P(None, 'node'), may hold values from 0 to 63, as said below
- tile_ids: int32 [3, 256], P(None, 'node'), may hold values from 0 to 7
- tile_count: int32 [3, 32], P(None, 'node'), may hold values from 4 to 8, as said below
Outputs:
- act_grads: bfloat16 [8, 3, 8192, 512], P('section', None, 'node')
- w_in_grad: float32 [8, 512, 1024], P('section')
- w_out_grad: float32 [8, 1024, 512], P('section')
The draws below stay inside these ranges and needn't reach their ends.
Inputs may be any that keep to these rules, and one draw needn't show every extreme that they name: `tile_cols`: A tile slot's column block lies on its own device or on the next or previous device along node, wrapping around; of one device's 8 slots at most 2 have columns on the next device and at most 2 on the previous one, and in every group some device has exactly 2 live slots with columns on the next device. Slots k < tile_count of a device are live; in every group some device has 8.
All inputs are finite; a program needn't handle non-finite values.
Results may differ from the reference program's by a relative error of at most 0.03.
Values may be sent and summed in bfloat16 or wider, within the bound.
No kernel may reach another device: no remote copies, remote signals or barrier semaphores. Data moves between devices by JAX's collectives and lax.ppermute only.
A program may use at most 64 MiB of HBM per device.

```python
import jax
import jax.numpy as jnp

D = 512
H = 1024
BLK = 128
ROWS = 256
GROUPS = 3
TD = 8
CAP = 2
TABLE = 8
NODES = 8192
LAYERS = 8
N_NODE = 32


def tile_plan(key):
    key = jax.random.fold_in(key, 11)
    devices = NODES // ROWS
    per_device = ROWS // BLK
    keys = jax.random.split(key, 6)
    shape_three = (GROUPS, devices, TD)
    row_pick = jax.random.randint(keys[0], shape_three, 0, per_device)
    direction = jax.random.randint(keys[1], shape_three, 0, 3)
    chosen = jax.random.randint(keys[2], (GROUPS, 1, 1), 0, devices)
    dev_index = jnp.arange(devices, dtype=jnp.int32)[None, :, None]
    slot_index = jnp.arange(TD, dtype=jnp.int32)
    direction = jnp.where((dev_index == chosen) & (slot_index[None, None, :] < CAP), 1, direction)
    earlier = slot_index[None, :] < slot_index[:, None]
    same_dir = direction[..., :, None] == direction[..., None, :]
    ranking = jnp.sum((same_dir & earlier[None, None]).astype(jnp.int32), axis=-1)
    direction = jnp.where((direction > 0) & (ranking >= CAP), 0, direction)
    counts = jax.random.randint(keys[3], (GROUPS, devices), TD // 2, TD + 1)
    counts = jnp.where(jnp.arange(devices)[None, :] == chosen[:, :, 0], TD, counts)
    offset = jnp.where(direction == 1, 1, jnp.where(direction == 2, devices - 1, 0))
    target = (dev_index + offset) % devices
    col_pick = target * per_device + jax.random.randint(keys[4], shape_three, 0, per_device)
    id_pick = jax.random.randint(keys[5], shape_three, 0, TABLE)
    return (row_pick.reshape(GROUPS, devices * TD).astype(jnp.int32), col_pick.reshape(GROUPS, devices * TD).astype(jnp.int32), id_pick.reshape(GROUPS, devices * TD).astype(jnp.int32), counts.astype(jnp.int32))


def draw_tile_rows(key, part):
    return tile_plan(key)[0]


def draw_tile_cols(key, part):
    return tile_plan(key)[1]


def draw_tile_ids(key, part):
    return tile_plan(key)[2]


def draw_tile_count(key, part):
    return tile_plan(key)[3]


def level_of(own_key, extent, shards, low, top_value):
    def one(axis_at, shards_of):
        steps = jax.random.uniform(jax.random.fold_in(jax.random.fold_in(own_key, 6), axis_at), (shards_of,), jnp.float32, low / len(shards), top_value / len(shards))
        return jnp.repeat(jnp.exp(steps), extent[axis_at] // shards_of).reshape((-1,) + (1,) * (len(extent) - axis_at - 1))

    gain = one(*shards[0])
    for cut in shards[1:]:
        gain = gain * one(*cut)
    return gain


def gaussian(own_key, dims, scale, most, shards=(), held_as=jnp.bfloat16):
    result = jax.random.normal(own_key, dims, jnp.float32) * scale
    if len(shards) > 0:
        result = level_of(own_key, dims, shards, -0.22, 0.18) * result
    return jnp.clip(result, min=-most, max=most).astype(held_as)


def setup_inputs(seed: int = 0) -> dict:
    seeds = jax.random.split(jax.random.key(seed), 10)
    acts = gaussian(seeds[0], (LAYERS, GROUPS, NODES, D), 1.0, 6.0, ((0, 8), (2, 32)))
    top_grad = gaussian(seeds[1], (GROUPS, NODES, D), 1.0, 6.0, ((1, 32),))
    w_in = gaussian(seeds[2], (LAYERS, D, H), D ** -0.5, 0.25, ((0, 8),))
    w_out = gaussian(seeds[3], (LAYERS, H, D), H ** -0.5, 0.1875, ((0, 8),))
    tile_table = gaussian(seeds[4], (GROUPS, TABLE * N_NODE, BLK, BLK), (4 * BLK) ** -0.5, 0.25, ((1, 32),))
    tile_rows = draw_tile_rows(jax.random.fold_in(seeds[9], 71), 0)
    tile_cols = draw_tile_cols(jax.random.fold_in(seeds[9], 71), 0)
    tile_ids = draw_tile_ids(jax.random.fold_in(seeds[9], 71), 0)
    tile_count = draw_tile_count(jax.random.fold_in(seeds[9], 71), 0)
    return {"acts": acts, "top_grad": top_grad, "w_in": w_in, "w_out": w_out, "tile_table": tile_table, "tile_rows": tile_rows, "tile_cols": tile_cols, "tile_ids": tile_ids, "tile_count": tile_count}


def reference(acts, top_grad, w_in, w_out, tile_table, tile_rows, tile_cols, tile_ids, tile_count):
    block_count = NODES // BLK
    devices = NODES // ROWS
    per_device = ROWS // BLK
    slot_dev = jnp.arange(devices * TD, dtype=jnp.int32) // TD
    slot_pos = jnp.arange(devices * TD, dtype=jnp.int32) % TD
    grads_all = []
    first_sum = [jnp.zeros((D, H), jnp.float32) for layer_idx in range(LAYERS)]
    second_sum = [jnp.zeros((H, D), jnp.float32) for layer_idx in range(LAYERS)]
    for group_idx in range(GROUPS):
        live_mask = slot_pos < tile_count[group_idx][slot_dev]
        row_glob = (slot_dev * per_device + tile_rows[group_idx]).astype(jnp.int32)
        table_idx = (slot_dev * TABLE + tile_ids[group_idx]).astype(jnp.int32)
        tile_vals = tile_table[group_idx][table_idx].astype(jnp.float32)
        grad_now = top_grad[group_idx]
        per_layer = [None] * LAYERS
        for layer_idx in range(LAYERS - 1, -1, -1):
            pieces = grad_now.reshape(block_count, BLK, D)[row_glob].astype(jnp.float32)
            terms = jnp.einsum('kij,kid->kjd', tile_vals, pieces).astype(jnp.bfloat16)
            terms = jnp.where(live_mask[:, None, None], terms.astype(jnp.float32), 0.0)
            summed = jax.ops.segment_sum(terms, tile_cols[group_idx], num_segments=block_count)
            grad_mid = summed.reshape(NODES, D).astype(jnp.bfloat16)
            layer_in = acts[layer_idx, group_idx]
            pre = jnp.dot(layer_in, w_in[layer_idx], preferred_element_type=jnp.float32)
            sigma = jax.nn.sigmoid(pre)
            act_val = (pre * sigma).astype(jnp.bfloat16)
            second_sum[layer_idx] = second_sum[layer_idx] + jnp.dot(act_val.T, grad_mid, preferred_element_type=jnp.float32)
            dact = jnp.dot(grad_mid, w_out[layer_idx].T, preferred_element_type=jnp.float32)
            dpre = (dact * sigma * (1.0 + pre * (1.0 - sigma))).astype(jnp.bfloat16)
            first_sum[layer_idx] = first_sum[layer_idx] + jnp.dot(layer_in.T, dpre, preferred_element_type=jnp.float32)
            back = jnp.dot(dpre, w_in[layer_idx].T, preferred_element_type=jnp.float32)
            grad_now = (grad_now.astype(jnp.float32) + back).astype(jnp.bfloat16)
            per_layer[layer_idx] = grad_now
        grads_all.append(jnp.stack(per_layer))
    act_grads = jnp.stack(grads_all, axis=1)
    return act_grads, jnp.stack(first_sum), jnp.stack(second_sum)
```

```python
import jax
import jax.numpy as jnp
from jax import lax
from jax.experimental import pallas as pl
from jax.experimental.pallas import tpu as pltpu
from jax.sharding import PartitionSpec as P


F32 = jnp.float32
BF16 = jnp.bfloat16
VM = pl.BlockSpec(memory_space=pltpu.VMEM)
SM = pl.BlockSpec(memory_space=pltpu.SMEM)
PIECES = 4
COLS = 4


def call(body, outs, ins_smem, ins, scratch=(), aliases=None, flops=0, grant=24 << 20):
    size = sum(x.size * x.dtype.itemsize for x in ins) + sum(x.size * x.dtype.itemsize for x in outs)
    return pl.pallas_call(
        body,
        out_shape=outs,
        in_specs=[SM] * len(ins_smem) + [VM] * len(ins),
        out_specs=[VM] * len(outs),
        scratch_shapes=list(scratch),
        input_output_aliases=aliases or {},
        compiler_params=pltpu.CompilerParams(vmem_limit_bytes=grant),
        cost_estimate=pl.CostEstimate(flops=flops, bytes_accessed=size, transcendentals=0),
    )(*ins_smem, *ins)


def struct(shape, dtype):
    return jax.ShapeDtypeStruct(shape, dtype)


def mm(a, b, contract):
    return lax.dot_general(a, b, ((contract[0], contract[1]), ((), ())), preferred_element_type=F32)


def shards(acts, top_grad, w_in, w_out, tile_table, tile_rows, tile_cols, tile_ids, tile_count):
    sections = lax.axis_size("section")
    nodes = lax.axis_size("node")
    place = jnp.stack([lax.axis_index("section"), lax.axis_index("node")]).astype(jnp.int32)
    groups, rows, dim = top_grad.shape
    table_size, blk = tile_table.shape[1], tile_table.shape[2]
    per = rows // blk
    slots = tile_rows.shape[1]
    hidden = w_in.shape[2]
    part = hidden // PIECES
    x_in, w1, w2 = acts[0], w_in[0], w_out[0]
    last = sections - 1

    def send(block, moves):
        return lax.ppermute(block, ("section", "node"), moves)

    def route(members, down, shift):
        return [
            (s * nodes + n, (s - down) * nodes + (n + shift) % nodes)
            for s in members
            for n in range(nodes)
        ]

    def adjacency(meta, place_ref, table, top, own, ahead, behind, *rest):
        terms, acc = rest[:-1], rest[-1]
        acc[...] = jnp.zeros(acc.shape, F32)

        def slot(i, carry):
            g, k = i // slots, i % slots

            @pl.when(k < meta[g, 3 * slots])
            def _():
                c = meta[g, slots + k]
                away = (c // per - place_ref[1] + nodes) % nodes
                target = jnp.where(away == 0, 0, jnp.where(away == 1, 1, 2))
                tile = table[g, meta[g, 2 * slots + k]].astype(F32)
                acc[g, target, c % per, meta[g, k]] += tile.T

            return carry

        lax.fori_loop(0, groups * slots, slot, 0)
        for g in range(groups):
            for t, ref in enumerate((own, ahead, behind)):
                for c in range(per):
                    for r in range(per):
                        ref[g, c * blk : (c + 1) * blk, r * blk : (r + 1) * blk] = acc[g, t, c, r].astype(BF16)

        @pl.when(place_ref[0] == last)
        def _():
            for g in range(groups):
                for i, ref in enumerate((ahead, behind)):
                    terms[2 * g + i][...] = mm(ref[g], top[g], ((1,), (0,))).astype(BF16)

    adj_shape = struct((groups, rows, rows), BF16)
    adj_own, adj_ahead, adj_behind, *terms = call(
        adjacency,
        [adj_shape] * 3 + [struct((rows, dim), BF16)] * (2 * groups),
        [jnp.concatenate([tile_rows, tile_cols, tile_ids, tile_count], axis=1), place],
        [tile_table, top_grad],
        [pltpu.VMEM((groups, 3, per, per, blk, blk), F32)],
    )

    def exchange(t, after):
        pair = lax.optimization_barrier((*terms[2 * t : 2 * t + 2], *after))[:2]
        return [send(v, route([last], 0, shift)) for v, shift in zip(pair, (1, -1))]

    adj_prev = send(adj_ahead, route(range(last), 0, 1))
    adj_next = send(adj_behind, route(range(last), 0, -1))

    def prepare(x_ref, w_ref, act_ref, slope_ref):
        def one(g, carry):
            x = x_ref[g]
            for j in range(PIECES):
                cut = slice(j * part, (j + 1) * part)
                pre = mm(x, w_ref[:, cut], ((1,), (0,)))
                sig = 1.0 / (1.0 + jnp.exp(-pre))
                act_ref[g, :, cut] = (pre * sig).astype(BF16)
                slope_ref[g, :, cut] = sig * (1.0 + pre * (1.0 - sig))
            return carry

        lax.fori_loop(0, groups, one, 0)

    act, slope = call(
        prepare,
        [struct((groups, rows, hidden), BF16), struct((groups, rows, hidden), F32)],
        [],
        [x_in, w1],
        flops=2 * groups * rows * dim * hidden,
    )

    def group_of(place_ref, t):
        g = t - (last - place_ref[0])
        return jnp.clip(g, 0, groups - 1), (g >= 0) & (g < groups)

    def back(t, lower, sides, after):
        top = t < groups

        def body(place_ref, *refs):
            own, w1_ref, w2_ref, slope_ref = refs[:4]
            g_out, dm_out, dpre_out, base, total = refs[-5:]
            refs = list(refs[4 + len(after) : -5])
            g, active = group_of(place_ref, t)
            if top:
                top_ref, side_a, side_b = refs[:3]
                refs = refs[3:]

                @pl.when(place_ref[0] == last)
                def _():
                    base[...] = top_ref[t]
                    total[...] = side_a[...].astype(F32) + side_b[...].astype(F32)

            if lower:
                prev, nxt, in_own, in_prev, in_next = refs

                @pl.when(active & (place_ref[0] != last))
                def _():
                    base[...] = in_own[...]
                    total[...] = mm(prev[g], in_prev[...], ((1,), (0,))) + mm(nxt[g], in_next[...], ((1,), (0,)))

            @pl.when(active)
            def _():
                dm = (total[...] + mm(own[g], base[...], ((1,), (0,)))).astype(BF16)
                dm_out[...] = dm
                out = base[...].astype(F32)
                for j in range(PIECES):
                    cut = slice(j * part, (j + 1) * part)
                    dact = mm(dm, w2_ref[cut, :], ((1,), (1,)))
                    dpre = (dact * slope_ref[g, :, cut]).astype(BF16)
                    dpre_out[:, cut] = dpre
                    out += mm(dpre, w1_ref[:, cut], ((1,), (1,)))
                g_out[...] = out.astype(BF16)

        ins = [adj_own, w1, w2, slope, *after]
        if top:
            ins += [top_grad, *exchange(t, after)]
        if lower:
            ins += [adj_prev, adj_next, *sides]
        return call(
            body,
            [struct((rows, dim), BF16), struct((rows, dim), BF16), struct((rows, hidden), BF16)],
            [place],
            ins,
            [pltpu.VMEM((rows, dim), BF16), pltpu.VMEM((rows, dim), F32)],
            flops=2 * rows * dim * (3 * rows + 2 * hidden),
        )

    def weights(t, dm, dpre, state):
        def body(place_ref, act_ref, x_ref, dm_ref, dpre_ref, *refs):
            first, second, _ = refs[-3:]
            before = refs[:-3]
            g, active = group_of(place_ref, t)

            @pl.when(active)
            def _():
                def piece(j, carry):
                    cut = pl.ds(pl.multiple_of(j * part, part), part)
                    a = mm(x_ref[g], dpre_ref[:, cut], ((0,), (0,)))
                    b = mm(act_ref[g, :, cut], dm_ref[...], ((0,), (0,)))
                    if before:
                        a += jnp.where(g == 0, 0.0, before[0][:, cut])
                        b += jnp.where(g == 0, 0.0, before[1][cut, :])
                    first[:, cut] = a
                    second[cut, :] = b
                    return carry

                lax.fori_loop(0, PIECES, piece, 0)

        outs = [
            struct((dim, hidden), F32),
            struct((hidden, dim), F32),
            struct((8, 128), F32),
        ]
        return call(
            body,
            outs,
            [place],
            [act, x_in, dm, dpre, *state],
            aliases={5 + i: i for i in range(len(state))},
            flops=4 * rows * dim * hidden,
        )

    def collect(place_ref, *refs):
        out = refs[-1]
        for t, ref in enumerate(refs[:-1]):
            g, active = group_of(place_ref, t)

            @pl.when(active)
            def _(ref=ref, g=g):
                out[g] = ref[...]

    state, done, after = [], [], []
    for t in range(groups + sections - 1):
        lower = [s for s in range(last) if 0 <= t - (last - s) < groups]
        up = [s + 1 for s in lower]
        sides = [send(done[-1], route(up, 1, shift)) for shift in (0, 1, -1)] if lower else []
        carried, dm, dpre = back(t, lower, sides, after)
        done.append(carried)
        *state, token = weights(t, dm, dpre, state)
        after = [token]
    first, second = state
    [grads] = call(collect, [struct((groups, rows, dim), BF16)], [place], done)

    ring = nodes // COLS
    along_x = [[x * ring + z for x in range(COLS)] for z in range(ring)]
    along_z = [[x * ring + z for z in range(ring)] for x in range(COLS)]
    half = hidden // 2
    a_rows, b_rows = dim // COLS, hidden // COLS
    flat = 2 * a_rows + b_rows
    fine = flat // ring

    def spread(first_ref, second_ref, out):
        for x in range(COLS):
            out[x, :b_rows] = second_ref[x * b_rows : (x + 1) * b_rows, :].astype(BF16)
            for i in range(2):
                piece = first_ref[x * a_rows : (x + 1) * a_rows, i * half : (i + 1) * half]
                out[x, b_rows + i * a_rows : b_rows + (i + 1) * a_rows] = piece.astype(BF16)

    def add_x(parts, out):
        for z in range(ring):
            cut = slice(z * fine, (z + 1) * fine)
            value = parts[0, cut].astype(F32)
            for x in range(1, COLS):
                value += parts[x, cut].astype(F32)
            out[z] = value.astype(BF16)

    def add_z(parts, out):
        value = parts[0].astype(F32)
        for z in range(1, ring):
            value += parts[z].astype(F32)
        value = value.astype(BF16)
        for z in range(ring):
            out[z] = value

    def join_z(parts, out):
        for x in range(COLS):
            for z in range(ring):
                out[x, z * fine : (z + 1) * fine] = parts[z]

    def whole(parts, first_ref, second_ref):
        for x in range(COLS):
            second_ref[x * b_rows : (x + 1) * b_rows, :] = parts[x, :b_rows].astype(F32)
            for i in range(2):
                piece = parts[x, b_rows + i * a_rows : b_rows + (i + 1) * a_rows]
                first_ref[x * a_rows : (x + 1) * a_rows, i * half : (i + 1) * half] = piece.astype(F32)

    def swap(block, members):
        return lax.all_to_all(block, "node", 0, 0, axis_index_groups=members)

    coarse_shape, fine_shape = struct((COLS, flat, dim), BF16), struct((ring, fine, dim), BF16)
    [packed] = call(spread, [coarse_shape], [], [first, second])
    [parts] = call(add_x, [fine_shape], [], [swap(packed, along_x)])
    [parts] = call(add_z, [fine_shape], [], [swap(parts, along_z)])
    [parts] = call(join_z, [coarse_shape], [], [swap(parts, along_z)])
    first, second = call(
        whole, [struct((dim, hidden), F32), struct((hidden, dim), F32)], [], [swap(parts, along_x)]
    )
    return (grads[None], first[None], second[None])


def solution(mesh):
    return jax.shard_map(
        shards,
        mesh=mesh,
        in_specs=(
            P("section", None, "node", None),
            P(None, "node", None),
            P("section", None, None),
            P("section", None, None),
            P(None, "node", None, None),
            P(None, "node"),
            P(None, "node"),
            P(None, "node"),
            P(None, "node"),
        ),
        out_specs=(
            P("section", None, "node", None),
            P("section", None, None),
            P("section", None, None),
        ),
        check_vma=False,
    )
```

```python
import jax
import jax.numpy as jnp
from jax import lax
from jax.experimental import pallas as pl
from jax.experimental.pallas import tpu as pltpu
from jax.sharding import PartitionSpec as P


F32 = jnp.float32
BF16 = jnp.bfloat16
VM = pl.BlockSpec(memory_space=pltpu.VMEM)
SM = pl.BlockSpec(memory_space=pltpu.SMEM)
FAR = pl.BlockSpec(memory_space=pltpu.HBM)
PIECES = 4
COLS = 4


def call(body, outs, ins_smem, ins, scratch=(), aliases=None, flops=0, far=0):
    size = sum(x.size * x.dtype.itemsize for x in ins) + sum(x.size * x.dtype.itemsize for x in outs)
    return pl.pallas_call(
        body,
        out_shape=outs,
        in_specs=[SM] * len(ins_smem) + [FAR if i == far - 1 else VM for i in range(len(ins))],
        out_specs=[FAR if far and i == 0 else VM for i in range(len(outs))],
        scratch_shapes=list(scratch),
        input_output_aliases=aliases or {},
        compiler_params=pltpu.CompilerParams(vmem_limit_bytes=24 << 20),
        cost_estimate=pl.CostEstimate(flops=flops, bytes_accessed=size, transcendentals=0),
    )(*ins_smem, *ins)


def struct(shape, dtype):
    return jax.ShapeDtypeStruct(shape, dtype)


def mm(a, b, contract):
    return lax.dot_general(a, b, ((contract[0], contract[1]), ((), ())), preferred_element_type=F32)


def shards(acts, top_grad, w_in, w_out, tile_table, tile_rows, tile_cols, tile_ids, tile_count):
    sections = lax.axis_size("section")
    nodes = lax.axis_size("node")
    place = jnp.stack([lax.axis_index("section"), lax.axis_index("node")]).astype(jnp.int32)
    groups, rows, dim = top_grad.shape
    table_size, blk = tile_table.shape[1], tile_table.shape[2]
    per = rows // blk
    slots = tile_rows.shape[1]
    hidden = w_in.shape[2]
    part = hidden // PIECES
    x_in, w1, w2 = acts[0], w_in[0], w_out[0]
    last = sections - 1

    def send(block, moves):
        return lax.ppermute(block, ("section", "node"), moves)

    def route(members, down, shift):
        return [
            (s * nodes + n, (s - down) * nodes + (n + shift) % nodes)
            for s in members
            for n in range(nodes)
        ]

    def adjacency(meta, place_ref, table, top, own, ahead, behind, *rest):
        terms, acc = rest[:-1], rest[-1]
        acc[...] = jnp.zeros(acc.shape, F32)

        def slot(i, carry):
            g, k = i // slots, i % slots

            @pl.when(k < meta[g, 3 * slots])
            def _():
                c = meta[g, slots + k]
                away = (c // per - place_ref[1] + nodes) % nodes
                target = jnp.where(away == 0, 0, jnp.where(away == 1, 1, 2))
                tile = table[g, meta[g, 2 * slots + k]].astype(F32)
                acc[g, target, c % per, meta[g, k]] += tile.T

            return carry

        lax.fori_loop(0, groups * slots, slot, 0)
        for g in range(groups):
            for t, ref in enumerate((own, ahead, behind)):
                for c in range(per):
                    for r in range(per):
                        ref[g, c * blk : (c + 1) * blk, r * blk : (r + 1) * blk] = acc[g, t, c, r].astype(BF16)

        @pl.when(place_ref[0] == last)
        def _():
            for g in range(groups):
                for i, ref in enumerate((ahead, behind)):
                    terms[i][g] = mm(ref[g], top[g], ((1,), (0,))).astype(BF16)

    adj_shape = struct((groups, rows, rows), BF16)
    adj_own, adj_ahead, adj_behind, *terms = call(
        adjacency,
        [adj_shape] * 3 + [struct((groups, rows, dim), BF16)] * 2,
        [jnp.concatenate([tile_rows, tile_cols, tile_ids, tile_count], axis=1), place],
        [tile_table, top_grad],
        [pltpu.VMEM((groups, 3, per, per, blk, blk), F32)],
    )

    top_sides = [send(v, route([last], 0, shift)) for v, shift in zip(terms, (1, -1))]

    def prepare(x_ref, w_ref, act_ref, flip_ref, slope_ref):
        def one(g, carry):
            x = x_ref[g]
            for j in range(dim // part):
                cut = slice(j * part, (j + 1) * part)
                flip_ref[g, cut, :] = x_ref[g, :, cut].astype(F32).T.astype(BF16)
            for j in range(PIECES):
                cut = slice(j * part, (j + 1) * part)
                pre = mm(x, w_ref[:, cut], ((1,), (0,)))
                sig = 1.0 / (1.0 + jnp.exp(-pre))
                act_ref[g, cut, :] = (pre * sig).T.astype(BF16)
                slope_ref[g, :, cut] = sig * (1.0 + pre * (1.0 - sig))
            return carry

        lax.fori_loop(0, groups, one, 0)

    act, flip, slope = call(
        prepare,
        [
            struct((groups, hidden, rows), BF16),
            struct((groups, dim, rows), BF16),
            struct((groups, rows, hidden), F32),
        ],
        [],
        [x_in, w1],
        flops=2 * groups * rows * dim * hidden,
    )
    def group_of(place_ref, t):
        g = t - (last - place_ref[0])
        return jnp.clip(g, 0, groups - 1), (g >= 0) & (g < groups)

    def back(t, lower, sides, after, adj):
        top = t < groups

        def body(place_ref, *refs):
            own, w1_ref, w2_ref, slope_ref = refs[:4]
            g_out, dm_out, dpre_out, base, total = refs[-5:]
            refs = list(refs[4 + len(after) : -5])
            g, active = group_of(place_ref, t)
            if top:
                top_ref, side_a, side_b = refs[:3]
                refs = refs[3:]

                @pl.when(place_ref[0] == last)
                def _():
                    base[...] = top_ref[t]
                    total[...] = side_a[t].astype(F32) + side_b[t].astype(F32)

            if lower:
                prev, nxt, in_own, in_prev, in_next = refs

                @pl.when(active & (place_ref[0] != last))
                def _():
                    base[...] = in_own[...]
                    total[...] = mm(prev[g], in_prev[...], ((1,), (0,))) + mm(nxt[g], in_next[...], ((1,), (0,)))

            @pl.when(active)
            def _():
                dm = (total[...] + mm(own[g], base[...], ((1,), (0,)))).astype(BF16)
                dm_out[...] = dm
                out = base[...].astype(F32)
                for j in range(PIECES):
                    cut = slice(j * part, (j + 1) * part)
                    dact = mm(dm, w2_ref[cut, :], ((1,), (1,)))
                    dpre = (dact * slope_ref[g, :, cut]).astype(BF16)
                    dpre_out[:, cut] = dpre
                    out += mm(dpre, w1_ref[:, cut], ((1,), (1,)))
                g_out[...] = out.astype(BF16)

        ins = [adj_own, w1, w2, slope, *after]
        if top:
            ins += [top_grad, *top_sides]
        if lower:
            ins += [*adj, *sides]
        return call(
            body,
            [struct((rows, dim), BF16), struct((rows, dim), BF16), struct((rows, hidden), BF16)],
            [place],
            ins,
            [pltpu.VMEM((rows, dim), BF16), pltpu.VMEM((rows, dim), F32)],
            flops=2 * rows * dim * (3 * rows + 2 * hidden),
        )

    half = hidden // 2
    flat = hidden + 2 * dim

    def weights(t, g_new, dm, dpre, state):
        final = t == groups + sections - 2

        def body(place_ref, grads_in, act_ref, flip_ref, g_ref, dm_ref, dpre_ref, *refs):
            before, (grads_ref, *outs, sem) = refs[: len(state) - 1], refs[len(state) - 1 :]
            g, active = group_of(place_ref, t)
            store = pltpu.make_async_copy(g_ref, grads_ref.at[g], sem)
            pl.when(active)(store.start)

            def fresh_a(cut):
                return mm(flip_ref[g], dpre_ref[:, cut], ((1,), (0,)))

            def fresh_b(cut):
                return mm(act_ref[g, cut, :], dm_ref[...], ((1,), (0,)))

            if final:

                def put(add):
                    for j in range(PIECES):
                        cut = slice(j * part, (j + 1) * part)
                        value = before[1][cut, :]
                        if add:
                            value += fresh_b(cut)
                        outs[0][cut, :] = value.astype(BF16)
                    for j in range(PIECES):
                        cut = slice(j * part, (j + 1) * part)
                        value = before[0][:, cut]
                        if add:
                            value += fresh_a(cut)
                        at = hidden + j * part // half * dim
                        low = j * part % half
                        outs[0][at : at + dim, low : low + part] = value.astype(BF16)

                pl.when(active)(lambda: put(True))
                pl.when(jnp.logical_not(active))(lambda: put(False))
                pl.when(active)(store.wait)
                return

            @pl.when(active)
            def _():
                def piece(j, carry):
                    cut = pl.ds(pl.multiple_of(j * part, part), part)
                    a, b = fresh_a(cut), fresh_b(cut)
                    if before:
                        a += jnp.where(g == 0, 0.0, before[0][:, cut])
                        b += jnp.where(g == 0, 0.0, before[1][cut, :])
                    outs[0][:, cut] = a
                    outs[1][cut, :] = b
                    return carry

                lax.fori_loop(0, PIECES, piece, 0)
                store.wait()

        outs = [struct((dim, hidden), F32), struct((hidden, dim), F32), struct((8, 128), F32)]
        return call(
            body,
            [struct((groups, rows, dim), BF16)] + ([struct((flat, dim), BF16)] if final else outs),
            [place],
            [state[0], act, flip, g_new, dm, dpre, *state[1:]],
            [pltpu.SemaphoreType.DMA],
            aliases={1: 0} if final else {1: 0, **{6 + i: i for i in range(1, len(state))}},
            flops=4 * rows * dim * hidden,
            far=1,
        )

    state, carried, after, adj = [jnp.zeros((groups, rows, dim), BF16)], None, [], None
    for t in range(groups + sections - 1):
        lower = [s for s in range(last) if 0 <= t - (last - s) < groups]
        up = [s + 1 for s in lower]
        sides = [send(carried, route(up, 1, shift)) for shift in (0, 1, -1)] if lower else []
        if t == 1:
            ahead, behind, _ = lax.optimization_barrier((adj_ahead, adj_behind, carried))
            adj = (send(ahead, route(range(last), 0, 1)), send(behind, route(range(last), 0, -1)))
        carried, dm, dpre = back(t, lower, sides, after, adj)
        *state, token = weights(t, carried, dm, dpre, state)
        after = [token]
    [grads], packed = state, token

    ring = nodes // COLS
    along_x = [[x * ring + z for x in range(COLS)] for z in range(ring)]
    along_z = [[x * ring + z for z in range(ring)] for x in range(COLS)]

    def reduced(order):
        (n1, wide), (n2, thin) = [(len(members[0]), members) for members in order]
        size = flat // n1
        fine = size // n2

        def swap(block, members):
            return lax.all_to_all(block, "node", 0, 0, axis_index_groups=members)

        def add_wide(parts, out):
            for i in range(n2):
                cut = slice(i * fine, (i + 1) * fine)
                value = parts[0, cut].astype(F32)
                for k in range(1, n1):
                    value += parts[k, cut].astype(F32)
                out[i] = value.astype(BF16)

        def add_thin(parts, out):
            value = parts[0].astype(F32)
            for k in range(1, n2):
                value += parts[k].astype(F32)
            value = value.astype(BF16)
            for k in range(n2):
                out[k] = value

        def join(parts, out):
            for i in range(n2):
                value = parts[i]
                for k in range(n1):
                    out[k, i * fine : (i + 1) * fine] = value

        def run(block):
            [block] = call(add_wide, [struct((n2, fine, dim), BF16)], [], [swap(block.reshape(n1, size, dim), wide)])
            [block] = call(add_thin, [struct((n2, fine, dim), BF16)], [], [swap(block, thin)])
            [block] = call(join, [struct((n1, size, dim), BF16)], [], [swap(block, thin)])
            return swap(block, wide).reshape(flat, dim)

        return run

    def whole(parts, first_ref, second_ref):
        for at in range(0, hidden, 128):
            second_ref[at : at + 128, :] = parts[at : at + 128, :].astype(F32)
        for at in range(0, dim, 128):
            for i in range(2):
                low = hidden + i * dim + at
                first_ref[at : at + 128, i * half : (i + 1) * half] = parts[low : low + 128, :].astype(F32)

    parts = reduced((along_x, along_z))(packed)
    first, second = call(whole, [struct((dim, hidden), F32), struct((hidden, dim), F32)], [], [parts])
    return (grads[None], first[None], second[None])


def solution(mesh):
    return jax.shard_map(
        shards,
        mesh=mesh,
        in_specs=(
            P("section", None, "node", None),
            P(None, "node", None),
            P("section", None, None),
            P("section", None, None),
            P(None, "node", None, None),
            P(None, "node"),
            P(None, "node"),
            P(None, "node"),
            P(None, "node"),
        ),
        out_specs=(
            P("section", None, "node", None),
            P("section", None, None),
            P("section", None, None),
        ),
        check_vma=False,
    )
```

```python
import jax
import jax.numpy as jnp
from jax import lax
from jax.experimental import pallas as pl
from jax.experimental.pallas import tpu as pltpu
from jax.sharding import PartitionSpec as P


F32 = jnp.float32
BF16 = jnp.bfloat16
VM = pl.BlockSpec(memory_space=pltpu.VMEM)
SM = pl.BlockSpec(memory_space=pltpu.SMEM)
FAR = pl.BlockSpec(memory_space=pltpu.HBM)
PIECES = 4
COLS = 4


def call(body, outs, ins_smem, ins, scratch=(), aliases=None, flops=0, far=0):
    size = sum(x.size * x.dtype.itemsize for x in ins) + sum(x.size * x.dtype.itemsize for x in outs)
    return pl.pallas_call(
        body,
        out_shape=outs,
        in_specs=[SM] * len(ins_smem) + [FAR if i == far - 1 else VM for i in range(len(ins))],
        out_specs=[FAR if far < 0 or (far and i == 0) else VM for i in range(len(outs))],
        scratch_shapes=list(scratch),
        input_output_aliases=aliases or {},
        compiler_params=pltpu.CompilerParams(vmem_limit_bytes=24 << 20),
        cost_estimate=pl.CostEstimate(flops=flops, bytes_accessed=size, transcendentals=0),
    )(*ins_smem, *ins)


def struct(shape, dtype):
    return jax.ShapeDtypeStruct(shape, dtype)


def mm(a, b, contract):
    return lax.dot_general(a, b, ((contract[0], contract[1]), ((), ())), preferred_element_type=F32)


def shards(acts, top_grad, w_in, w_out, tile_table, tile_rows, tile_cols, tile_ids, tile_count):
    sections = lax.axis_size("section")
    nodes = lax.axis_size("node")
    place = jnp.stack([lax.axis_index("section"), lax.axis_index("node")]).astype(jnp.int32)
    groups, rows, dim = top_grad.shape
    table_size, blk = tile_table.shape[1], tile_table.shape[2]
    per = rows // blk
    slots = tile_rows.shape[1]
    hidden = w_in.shape[2]
    part = hidden // PIECES
    x_in, w1, w2 = acts[0], w_in[0], w_out[0]
    last = sections - 1

    def send(block, moves):
        return lax.ppermute(block, ("section", "node"), moves)

    def route(members, down, shift):
        return [
            (s * nodes + n, (s - down) * nodes + (n + shift) % nodes)
            for s in members
            for n in range(nodes)
        ]

    def adjacency(meta, place_ref, table, top, own, ahead, behind, *rest):
        terms, acc = rest[:-1], rest[-1]
        acc[...] = jnp.zeros(acc.shape, F32)

        def slot(i, carry):
            g, k = i // slots, i % slots

            @pl.when(k < meta[g, 3 * slots])
            def _():
                c = meta[g, slots + k]
                away = (c // per - place_ref[1] + nodes) % nodes
                target = jnp.where(away == 0, 0, jnp.where(away == 1, 1, 2))
                tile = table[g, meta[g, 2 * slots + k]].astype(F32)
                acc[g, target, c % per, meta[g, k]] += tile.T

            return carry

        lax.fori_loop(0, groups * slots, slot, 0)
        for g in range(groups):
            for t, ref in enumerate((own, ahead, behind)):
                for c in range(per):
                    for r in range(per):
                        ref[g, c * blk : (c + 1) * blk, r * blk : (r + 1) * blk] = acc[g, t, c, r].astype(BF16)

        @pl.when(place_ref[0] == last)
        def _():
            for g in range(groups):
                for i, ref in enumerate((ahead, behind)):
                    terms[i][g] = mm(ref[g], top[g], ((1,), (0,))).astype(BF16)

    adj_shape = struct((groups, rows, rows), BF16)
    adj_own, adj_ahead, adj_behind, *terms = call(
        adjacency,
        [adj_shape] * 3 + [struct((groups, rows, dim), BF16)] * 2,
        [jnp.concatenate([tile_rows, tile_cols, tile_ids, tile_count], axis=1), place],
        [tile_table, top_grad],
        [pltpu.VMEM((groups, 3, per, per, blk, blk), F32)],
    )

    top_sides = [send(v, route([last], 0, shift)) for v, shift in zip(terms, (1, -1))]

    def prepare(x_ref, w_ref, act_ref, flip_ref, slope_ref):
        def one(g, carry):
            x = x_ref[g]
            for j in range(dim // part):
                cut = slice(j * part, (j + 1) * part)
                flip_ref[g, cut, :] = x_ref[g, :, cut].astype(F32).T.astype(BF16)
            for j in range(PIECES):
                cut = slice(j * part, (j + 1) * part)
                pre = mm(x, w_ref[:, cut], ((1,), (0,)))
                sig = 1.0 / (1.0 + jnp.exp(-pre))
                act_ref[g, cut, :] = (pre * sig).T.astype(BF16)
                slope_ref[g, :, cut] = sig * (1.0 + pre * (1.0 - sig))
            return carry

        lax.fori_loop(0, groups, one, 0)

    act, flip, slope = call(
        prepare,
        [
            struct((groups, hidden, rows), BF16),
            struct((groups, dim, rows), BF16),
            struct((groups, rows, hidden), F32),
        ],
        [],
        [x_in, w1],
        flops=2 * groups * rows * dim * hidden,
    )
    def group_of(place_ref, t):
        g = t - (last - place_ref[0])
        return jnp.clip(g, 0, groups - 1), (g >= 0) & (g < groups)

    def back(t, lower, sides, after, adj):
        top = t < groups

        def body(place_ref, *refs):
            own, w1_ref, w2_ref, slope_ref = refs[:4]
            g_out, dm_out, dpre_out, base, total = refs[-5:]
            refs = list(refs[4 + len(after) : -5])
            g, active = group_of(place_ref, t)
            if top:
                top_ref, side_a, side_b = refs[:3]
                refs = refs[3:]

                @pl.when(place_ref[0] == last)
                def _():
                    base[...] = top_ref[t]
                    total[...] = side_a[t].astype(F32) + side_b[t].astype(F32)

            if lower:
                prev, nxt, in_own, in_prev, in_next = refs

                @pl.when(active & (place_ref[0] != last))
                def _():
                    base[...] = in_own[...]
                    total[...] = mm(prev[g], in_prev[...], ((1,), (0,))) + mm(nxt[g], in_next[...], ((1,), (0,)))

            @pl.when(active)
            def _():
                dm = (total[...] + mm(own[g], base[...], ((1,), (0,)))).astype(BF16)
                dm_out[...] = dm
                out = base[...].astype(F32)
                for j in range(PIECES):
                    cut = slice(j * part, (j + 1) * part)
                    dact = mm(dm, w2_ref[cut, :], ((1,), (1,)))
                    dpre = (dact * slope_ref[g, :, cut]).astype(BF16)
                    dpre_out[:, cut] = dpre
                    out += mm(dpre, w1_ref[:, cut], ((1,), (1,)))
                g_out[...] = out.astype(BF16)

        ins = [adj_own, w1, w2, slope, *after]
        if top:
            ins += [top_grad, *top_sides]
        if lower:
            ins += [*adj, *sides]
        return call(
            body,
            [struct((rows, dim), BF16), struct((rows, dim), BF16), struct((rows, hidden), BF16)],
            [place],
            ins,
            [pltpu.VMEM((rows, dim), BF16), pltpu.VMEM((rows, dim), F32)],
            flops=2 * rows * dim * (3 * rows + 2 * hidden),
        )

    half = hidden // 2
    flat = hidden + 2 * dim

    def weights(t, g_new, dm, dpre, state):
        final = t == groups + sections - 2

        def body(place_ref, grads_in, act_ref, flip_ref, g_ref, dm_ref, dpre_ref, *refs):
            before, (grads_ref, *outs, sem) = refs[: len(state) - 1], refs[len(state) - 1 :]
            g, active = group_of(place_ref, t)
            store = pltpu.make_async_copy(g_ref, grads_ref.at[g], sem)
            pl.when(active)(store.start)

            def fresh_a(cut):
                return mm(flip_ref[g], dpre_ref[:, cut], ((1,), (0,)))

            def fresh_b(cut):
                return mm(act_ref[g, cut, :], dm_ref[...], ((1,), (0,)))

            if final:

                def put(add):
                    for j in range(PIECES):
                        cut = slice(j * part, (j + 1) * part)
                        value = before[1][cut, :]
                        if add:
                            value += fresh_b(cut)
                        outs[0][cut, :] = value.astype(BF16)
                    for j in range(PIECES):
                        cut = slice(j * part, (j + 1) * part)
                        value = before[0][:, cut]
                        if add:
                            value += fresh_a(cut)
                        at = hidden + j * part // half * dim
                        low = j * part % half
                        outs[0][at : at + dim, low : low + part] = value.astype(BF16)

                pl.when(active)(lambda: put(True))
                pl.when(jnp.logical_not(active))(lambda: put(False))
                pl.when(active)(store.wait)
                return

            @pl.when(active)
            def _():
                def piece(j, carry):
                    cut = pl.ds(pl.multiple_of(j * part, part), part)
                    a, b = fresh_a(cut), fresh_b(cut)
                    if before:
                        a += jnp.where(g == 0, 0.0, before[0][:, cut])
                        b += jnp.where(g == 0, 0.0, before[1][cut, :])
                    outs[0][:, cut] = a
                    outs[1][cut, :] = b
                    return carry

                lax.fori_loop(0, PIECES, piece, 0)
                store.wait()

        outs = [struct((dim, hidden), F32), struct((hidden, dim), F32), struct((8, 128), F32)]
        return call(
            body,
            [struct((groups, rows, dim), BF16)] + ([struct((flat, dim), BF16)] if final else outs),
            [place],
            [state[0], act, flip, g_new, dm, dpre, *state[1:]],
            [pltpu.SemaphoreType.DMA],
            aliases={1: 0} if final else {1: 0, **{6 + i: i for i in range(1, len(state))}},
            flops=4 * rows * dim * hidden,
            far=1,
        )

    state, carried, after, adj = [jnp.zeros((groups, rows, dim), BF16)], None, [], None
    for t in range(groups + sections - 1):
        lower = [s for s in range(last) if 0 <= t - (last - s) < groups]
        up = [s + 1 for s in lower]
        sides = [send(carried, route(up, 1, shift)) for shift in (0, 1, -1)] if lower else []
        if t == 1:
            ahead, behind, _ = lax.optimization_barrier((adj_ahead, adj_behind, carried))
            adj = (send(ahead, route(range(last), 0, 1)), send(behind, route(range(last), 0, -1)))
        carried, dm, dpre = back(t, lower, sides, after, adj)
        *state, token = weights(t, carried, dm, dpre, state)
        after = [token]
    [grads], packed = state, token

    ring = nodes // COLS
    along_x = [[x * ring + z for x in range(COLS)] for z in range(ring)]
    along_z = [[x * ring + z for z in range(ring)] for x in range(COLS)]

    def reduced(order):
        (n1, wide), (n2, thin) = [(len(members[0]), members) for members in order]
        size = flat // n1
        fine = size // n2

        def swap(block, members):
            return lax.all_to_all(block, "node", 0, 0, axis_index_groups=members)

        def add_wide(parts, out):
            for i in range(n2):
                cut = slice(i * fine, (i + 1) * fine)
                value = parts[0, cut].astype(F32)
                for k in range(1, n1):
                    value += parts[k, cut].astype(F32)
                out[i] = value.astype(BF16)

        def add_thin(parts, out):
            value = parts[0].astype(F32)
            for k in range(1, n2):
                value += parts[k].astype(F32)
            value = value.astype(BF16)
            for k in range(n2):
                out[k] = value

        def join(parts, out):
            for i in range(n2):
                value = parts[i]
                for k in range(n1):
                    out[k, i * fine : (i + 1) * fine] = value

        def run(block):
            [block] = call(add_wide, [struct((n2, fine, dim), BF16)], [], [swap(block.reshape(n1, size, dim), wide)])
            [block] = call(add_thin, [struct((n2, fine, dim), BF16)], [], [swap(block, thin)])
            [block] = call(join, [struct((n1, size, dim), BF16)], [], [swap(block, thin)])
            return swap(block, wide).reshape(flat, dim)

        return run

    def whole(parts, first_far, second_far, first_ref, second_ref, sems):
        copies = []

        def leave(ref, far, cut):
            copies.append(pltpu.make_async_copy(ref.at[cut, :], far.at[cut, :], sems.at[len(copies)]))
            copies[-1].start()

        for j in range(PIECES):
            size = hidden // PIECES
            cut = slice(j * size, (j + 1) * size)
            second_ref[cut, :] = parts[cut, :].astype(F32)
            leave(second_ref, second_far, pl.ds(j * size, size))
        for j in range(PIECES):
            size = dim // PIECES
            cut = slice(j * size, (j + 1) * size)
            for i in range(2):
                low = hidden + i * dim + j * size
                first_ref[cut, i * half : (i + 1) * half] = parts[low : low + size, :].astype(F32)
            leave(first_ref, first_far, pl.ds(j * size, size))
        for copy in copies:
            copy.wait()

    parts = reduced((along_x, along_z))(packed)
    first, second = call(
        whole,
        [struct((dim, hidden), F32), struct((hidden, dim), F32)],
        [],
        [parts],
        [
            pltpu.VMEM((dim, hidden), F32),
            pltpu.VMEM((hidden, dim), F32),
            pltpu.SemaphoreType.DMA((2 * PIECES,)),
        ],
        far=-1,
    )
    return (grads[None], first[None], second[None])


def solution(mesh):
    return jax.shard_map(
        shards,
        mesh=mesh,
        in_specs=(
            P("section", None, "node", None),
            P(None, "node", None),
            P("section", None, None),
            P("section", None, None),
            P(None, "node", None, None),
            P(None, "node"),
            P(None, "node"),
            P(None, "node"),
            P(None, "node"),
        ),
        out_specs=(
            P("section", None, "node", None),
            P("section", None, None),
            P("section", None, None),
        ),
        check_vma=False,
    )
```
